512 devices in a mesh: hot: 32 (over z_hi, x, core), load: 16 (over z_lo, y).
Axes of the slice: x: 4, y: 4, z: 16 (z_hi: 4, z_lo: 4; z = z_hi * 4 + z_lo), core: 2. Of those that a mesh axis runs over, the one named last changes fastest.
Arguments:
- response: bfloat16 [2048, 2048, 128], P('hot', 'load'), may hold values from -1 to 1, as said below
- forces: bfloat16 [2048, 1408], P('load'), may hold values from -6 to 6
- measured: float32 [2048, 384], P('hot'), may hold values from -6 to 6
Outputs:
- updated_forces: float32 [2048, 1408], P('load')
- updated_residual: float32 [2048, 384], P('hot')
The draws below stay inside these ranges and needn't reach their ends.
Inputs may be any that keep to these rules, and one draw needn't show every extreme that they name: impulse-response coefficients.
All inputs are finite; a program needn't handle non-finite values.
Results may differ from the reference program's by a relative error of at most 0.0041.
Values sent between devices are 32-bit elements; how exact they have to be, the bound alone decides.
No kernel may reach another device: no remote copies, remote signals or barrier semaphores. Data moves between devices by JAX's collectives and lax.ppermute only.
A program may use at most 128 MiB of HBM per device.

```python
import jax
import jax.numpy as jnp
from jax import lax

HOTSPOTS = 2048
LOADS = 2048
TAPS = 128
SEG = 48
CASES = 8
HIST = 128
STEPS = 176


def draw_response(key, part):
    shape = (HOTSPOTS, LOADS, TAPS)
    first_key = jax.random.fold_in(key, 0)
    hot_pos = jnp.arange(HOTSPOTS, dtype=jnp.float32)[:, None, None] / (HOTSPOTS - 1)
    load_pos = jnp.arange(LOADS, dtype=jnp.float32)[None, :, None] / (LOADS - 1)
    rising = jnp.exp(jnp.log(3.0) * (hot_pos + load_pos))
    base = jax.random.truncated_normal(first_key, -6.0, 6.0, shape, jnp.float32)
    values = base * rising
    values = values / (2.0 * jnp.sqrt(jnp.float32(LOADS * TAPS)))
    return values.astype(jnp.bfloat16)


def levels(own_key, dims, pieces, least, top_value):
    def one(position, shards_of):
        heights = jax.random.uniform(jax.random.fold_in(jax.random.fold_in(own_key, 6), position), (shards_of,), jnp.float32, least / len(pieces), top_value / len(pieces))
        return jnp.repeat(jnp.exp(heights), dims[position] // shards_of).reshape((-1,) + (1,) * (len(dims) - position - 1))

    level = one(*pieces[0])
    for cut in pieces[1:]:
        level = level * one(*cut)
    return level


def normal_values(own_key, shape, deviation, most, shards=(), held_as=jnp.bfloat16):
    level = levels(own_key, shape, shards, -0.22, 0.18) if shards else 1.0
    result = jax.random.normal(own_key, shape, jnp.float32) * deviation * level
    return jnp.minimum(jnp.maximum(result, -most), most).astype(held_as)


def setup_inputs(seed: int = 0) -> dict:
    key_of = jax.random.split(jax.random.key(seed), 4)
    response = draw_response(jax.random.fold_in(key_of[3], 71), 0)
    forces = normal_values(key_of[1], (LOADS, STEPS * CASES), 1.0, 6.0, ((0, 16),))
    measured = normal_values(key_of[2], (HOTSPOTS, SEG * CASES), 1.0, 6.0, ((0, 32),), jnp.float32)
    return dict(response=response, forces=forces, measured=measured)


def strain_product(response, signal):
    seg_cols = SEG * CASES
    running = jnp.zeros((response.shape[0], seg_cols), jnp.float32)
    tap_span = min(16, TAPS)
    for first_tap in range(0, TAPS, tap_span):
        tap_block = response[:, :, first_tap:first_tap + tap_span].astype(jnp.float32)
        window = jnp.stack([signal[:, (HIST - tap_index) * CASES:(HIST - tap_index) * CASES + seg_cols]
                            for tap_index in range(first_tap, first_tap + tap_span)], axis=1).astype(jnp.float32)
        running = running + jnp.einsum('hlk,lkm->hm', tap_block, window, precision=lax.Precision.HIGHEST)
    return running


def load_product(response, strains):
    col_count = STEPS * CASES
    padded = jnp.pad(strains.astype(jnp.float32), ((0, 0), (HIST * CASES, TAPS * CASES)))
    running = jnp.zeros((response.shape[1], col_count), jnp.float32)
    tap_span = min(16, TAPS)
    for first_tap in range(0, TAPS, tap_span):
        tap_block = response[:, :, first_tap:first_tap + tap_span].astype(jnp.float32)
        window = jnp.stack([padded[:, tap_index * CASES:tap_index * CASES + col_count]
                            for tap_index in range(first_tap, first_tap + tap_span)], axis=1)
        running = running + jnp.einsum('hlk,hkm->lm', tap_block, window, precision=lax.Precision.HIGHEST)
    return running


def reference(response, forces, measured):
    strains = strain_product(response, forces)
    residual = measured - strains
    residual_b = residual.astype(jnp.bfloat16)
    gradient = load_product(response, residual_b)
    gradient_b = gradient.astype(jnp.bfloat16)
    image_sum = strain_product(response, gradient_b)
    step_size = jnp.sum(gradient * gradient) / jnp.sum(image_sum * image_sum)
    return forces.astype(jnp.float32) + step_size * gradient, residual - step_size * image_sum
```

```python
import jax
import jax.numpy as jnp
from jax import lax
from jax.experimental import pallas as pl
from jax.experimental.pallas import tpu as pltpu
from jax.sharding import Mesh, PartitionSpec as P

TAPS = 128
SEG = 48
CASES = 8
HIST = 128
STEPS = 176
LANES = 128
PHASES = LANES // CASES
SPANS = TAPS // PHASES
SEG_COLS = SEG * CASES
SEG_BLOCKS = SEG_COLS // LANES
COLS = STEPS * CASES
BLOCKS = COLS // LANES
F32 = jnp.float32
BF16 = jnp.bfloat16
VMEM_LIMIT = 40 * 1024 * 1024


def fill_forward_weights(taps_ref, weights):
    hots = taps_ref.shape[1]
    for tap in range(TAPS):
        span, phase = divmod(tap, PHASES)
        weights[span * hots:(span + 1) * hots, phase * LANES:(phase + 1) * LANES] = taps_ref[tap]


def fill_adjoint_weights(taps_ref, weights):
    hots = taps_ref.shape[1]
    for tap in range(TAPS):
        span, phase = divmod(tap, PHASES)
        weights[phase * hots:(phase + 1) * hots, span * LANES:(span + 1) * LANES] = taps_ref[tap]


def forward_product(signal_t, taps_ref, windows, weights):
    hots = taps_ref.shape[1]
    fill_forward_weights(taps_ref, weights)
    rows = COLS - LANES
    for phase in range(PHASES):
        first = LANES - CASES * phase
        windows[:, phase * LANES:(phase + 1) * LANES] = signal_t[first:first + rows, :].astype(BF16)
    parts = [None] * SEG_BLOCKS
    for block in range(1, BLOCKS, 2):
        low = max(SPANS - 1 - block, 0)
        high = min(SPANS + 2 - block, SPANS - 1)
        out = lax.dot_general(
            windows[(block - 1) * LANES:(block + 1) * LANES, :],
            weights[low * hots:(high + 1) * hots, :],
            (((1,), (1,)), ((), ())),
            preferred_element_type=F32,
        )
        for half in range(2):
            for span in range(low, high + 1):
                target = block + half + span - SPANS
                if 0 <= target < SEG_BLOCKS:
                    piece = out[half * LANES:(half + 1) * LANES, (span - low) * hots:(span - low + 1) * hots]
                    parts[target] = piece if parts[target] is None else parts[target] + piece
    return jnp.concatenate(parts, axis=0)


def pack_strains(value, out_ref, scratch):
    half = SEG_COLS // 2
    hots = value.shape[1]
    scratch[:, 0:hots] = value[0:half]
    scratch[:, hots:2 * hots] = value[half:]
    chunks = out_ref.shape[0]
    size = half // chunks
    for chunk in range(chunks):
        out_ref[chunk, 0:size, :] = scratch[chunk * size:(chunk + 1) * size, :]


def unpack_strains(chunks_ref, scratch):
    chunks = chunks_ref.shape[0]
    size = (SEG_COLS // 2) // chunks
    for chunk in range(chunks):
        scratch[chunk * size:(chunk + 1) * size, :] = chunks_ref[chunk, 0:size, :]


def strain_kernel(taps_ref, forces_ref, measured_ref, part_ref, measured_t_ref, signal_t, windows, weights, packed):
    for block in range(BLOCKS):
        cols = slice(block * LANES, (block + 1) * LANES)
        signal_t[cols, :] = forces_ref[:, cols].astype(F32).T
    result = forward_product(signal_t, taps_ref, windows, weights)
    part_ref[...] = jnp.zeros_like(part_ref)
    pack_strains(result, part_ref, packed)
    half = SEG_COLS // 2
    hots = measured_ref.shape[0]
    measured_t = measured_ref[...].T
    measured_t_ref[:, 0:hots] = measured_t[0:half]
    measured_t_ref[:, hots:2 * hots] = measured_t[half:]


def gradient_kernel(taps_ref, strains_ref, measured_t_ref, part_ref, residual_ref, packed, padded, windows, weights, total):
    hots = taps_ref.shape[1]
    half = SEG_COLS // 2
    unpack_strains(strains_ref, packed)
    residual = measured_t_ref[...] - packed[...]
    residual_ref[...] = residual
    padded[...] = jnp.zeros_like(padded)
    for lane, shift in ((0, 0), (hots, CASES)):
        padded[LANES - shift:LANES - shift + half, lane:lane + hots] = residual[:, 0:hots]
        padded[LANES - shift + half:LANES - shift + 2 * half, lane:lane + hots] = residual[:, hots:2 * hots]
    fill_adjoint_weights(taps_ref, weights)
    rows = windows.shape[0]
    for pair in range(PHASES // 2):
        first = 2 * CASES * pair
        windows[:, pair * 2 * hots:(pair + 1) * 2 * hots] = padded[first:first + rows, :].astype(BF16)
    seen = set()
    for span in range(0, SPANS, 2):
        out = jnp.dot(windows[...], weights[:, span * LANES:(span + 2) * LANES], preferred_element_type=F32)
        for side in range(2):
            for row in range(rows // LANES):
                block = row - 1 + SPANS - (span + side)
                piece = out[row * LANES:(row + 1) * LANES, side * LANES:(side + 1) * LANES]
                cols = slice(block * LANES, (block + 1) * LANES)
                if block in seen:
                    total[cols, :] += piece
                else:
                    total[cols, :] = piece
                    seen.add(block)
    chunks = part_ref.shape[0]
    size = COLS // chunks
    for chunk in range(chunks):
        part_ref[chunk, 0:size, :] = total[chunk * size:(chunk + 1) * size, :]
        part_ref[chunk, size:, :] = jnp.zeros((part_ref.shape[1] - size, LANES), F32)


def image_kernel(taps_ref, gradient_ref, part_ref, signal_t, windows, weights, packed):
    chunks = gradient_ref.shape[0]
    size = COLS // chunks
    for chunk in range(chunks):
        signal_t[chunk * size:(chunk + 1) * size, :] = gradient_ref[chunk, 0:size, :]
    result = forward_product(signal_t, taps_ref, windows, weights)
    gradient = signal_t[...]
    squares = jnp.sum(gradient * gradient, axis=0, keepdims=True)
    pack_strains(result, part_ref, packed)
    size = (SEG_COLS // 2) // part_ref.shape[0]
    for chunk in range(part_ref.shape[0]):
        part_ref[chunk, size:, :] = jnp.broadcast_to(squares, (part_ref.shape[1] - size, LANES))


def update_kernel(forces_ref, gradient_ref, image_ref, residual_ref, forces_out, residual_out, signal_t, packed):
    size = (SEG_COLS // 2) // image_ref.shape[0]
    squares = image_ref[0, size:size + 1, :]
    image_squares = jnp.zeros((1, LANES), F32)
    for chunk in range(image_ref.shape[0]):
        image_squares = image_squares + image_ref[chunk, size + 1:size + 2, :]
    step_size = jnp.sum(squares, axis=1, keepdims=True) / jnp.sum(image_squares, axis=1, keepdims=True)
    unpack_strains(image_ref, packed)
    left = residual_ref[...] - step_size * packed[...]
    hots = residual_out.shape[0]
    half = SEG_COLS // 2
    left_t = jnp.concatenate([left[:, 0:hots], left[:, hots:2 * hots]], axis=0)
    residual_out[...] = left_t.T
    chunks = gradient_ref.shape[0]
    size = COLS // chunks
    for chunk in range(chunks):
        signal_t[chunk * size:(chunk + 1) * size, :] = gradient_ref[chunk, 0:size, :]
    for block in range(BLOCKS):
        cols = slice(block * LANES, (block + 1) * LANES)
        forces_out[:, cols] = forces_ref[:, cols].astype(F32) + step_size * signal_t[cols, :].T


def call(kernel, outs, scratch):
    return pl.pallas_call(
        kernel,
        out_shape=outs,
        scratch_shapes=scratch,
        compiler_params=pltpu.CompilerParams(vmem_limit_bytes=VMEM_LIMIT),
    )


def body(response, forces, measured):
    hots, loads, _ = response.shape
    load_axes, near_axes = ("zl", "y"), ("zh", "x")
    peers = lax.axis_size(load_axes)
    near = lax.axis_size(near_axes)
    hot_peers = near * lax.axis_size("c")
    half = SEG_COLS // 2
    chunk_rows = -(-(half // peers + 2) // 8) * 8
    grad_rows = -(-(COLS // hot_peers) // 8) * 8
    part = jax.ShapeDtypeStruct((peers, chunk_rows, LANES), F32)
    packed_shape = jax.ShapeDtypeStruct((half, 2 * hots), F32)
    forward_scratch = [
        pltpu.VMEM((COLS, loads), F32),
        pltpu.VMEM((COLS - LANES, PHASES * loads), BF16),
        pltpu.VMEM((SPANS * hots, PHASES * loads), BF16),
        pltpu.VMEM((half, 2 * hots), F32),
    ]

    def spread(value, count):
        return jnp.broadcast_to(value[None], (count,) + value.shape)

    taps = jnp.transpose(response, (2, 0, 1))
    strain_part, measured_t = call(strain_kernel, (part, packed_shape), forward_scratch)(taps, forces, measured)
    got = lax.all_to_all(strain_part, load_axes, 0, 0)
    strains = lax.all_to_all(spread(jnp.sum(got, axis=0), peers), load_axes, 0, 0)
    grad_part, residual = call(
        gradient_kernel,
        (jax.ShapeDtypeStruct((hot_peers, grad_rows, LANES), F32), packed_shape),
        [
            pltpu.VMEM((half, 2 * hots), F32),
            pltpu.VMEM((SEG_COLS + 2 * LANES, 2 * hots), F32),
            pltpu.VMEM((SEG_COLS + LANES, PHASES * hots), BF16),
            pltpu.VMEM((PHASES * hots, SPANS * loads), BF16),
            pltpu.VMEM((COLS, loads), F32),
        ],
    )(taps, strains, measured_t)
    got = lax.all_to_all(grad_part.reshape(2, near, grad_rows, LANES), "c", 0, 0)
    got = lax.all_to_all(got[0] + got[1], near_axes, 0, 0)
    got = lax.all_to_all(spread(jnp.sum(got, axis=0), near), near_axes, 0, 0)
    gradient = lax.all_to_all(spread(got, 2), "c", 0, 0).reshape(hot_peers, grad_rows, LANES)
    image_part = call(image_kernel, part, forward_scratch)(taps, gradient)
    image = jnp.sum(lax.all_to_all(image_part, load_axes, 0, 0), axis=0)
    rows = half // peers
    squares = jnp.sum(image[:rows] * image[:rows], axis=0, keepdims=True)
    squares = lax.all_to_all(spread(squares, hot_peers), ("zh", "x", "c"), 0, 0)
    squares = jnp.sum(squares, axis=0)
    image = jnp.concatenate([image[:rows + 1], squares, image[rows + 2:]], axis=0)
    image = lax.all_to_all(spread(image, peers), load_axes, 0, 0)
    return call(
        update_kernel,
        (jax.ShapeDtypeStruct((loads, COLS), F32), jax.ShapeDtypeStruct((hots, SEG_COLS), F32)),
        [pltpu.VMEM((COLS, loads), F32), pltpu.VMEM((half, 2 * hots), F32)],
    )(forces, gradient, image, residual)


def solution(mesh):
    parts = Mesh(mesh.devices.reshape(4, 4, 2, 4, 4), ("zh", "x", "c", "zl", "y"))
    hot, load = ("zh", "x", "c"), ("zl", "y")
    return jax.shard_map(
        body,
        mesh=parts,
        in_specs=(P(hot, load, None), P(load, None), P(hot, None)),
        out_specs=(P(load, None), P(hot, None)),
        check_vma=False,
    )
```

```python
import jax
import jax.numpy as jnp
from jax import lax
from jax.experimental import pallas as pl
from jax.experimental.pallas import tpu as pltpu
from jax.sharding import Mesh, PartitionSpec as P

TAPS = 128
SEG = 48
CASES = 8
HIST = 128
STEPS = 176
LANES = 128
PHASES = LANES // CASES
SPANS = TAPS // PHASES
SEG_COLS = SEG * CASES
SEG_BLOCKS = SEG_COLS // LANES
COLS = STEPS * CASES
BLOCKS = COLS // LANES
F32 = jnp.float32
BF16 = jnp.bfloat16
VMEM_LIMIT = 40 * 1024 * 1024


def fill_forward_weights(taps_ref, weights):
    hots = taps_ref.shape[1]
    for tap in range(TAPS):
        span, phase = divmod(tap, PHASES)
        weights[span * hots:(span + 1) * hots, phase * LANES:(phase + 1) * LANES] = taps_ref[tap]


def fill_adjoint_weights(taps_ref, weights):
    hots = taps_ref.shape[1]
    for tap in range(TAPS):
        span, phase = divmod(tap, PHASES)
        weights[phase * hots:(phase + 1) * hots, span * LANES:(span + 1) * LANES] = taps_ref[tap]


def forward_product(signal_t, taps_ref, windows, weights):
    hots = taps_ref.shape[1]
    fill_forward_weights(taps_ref, weights)
    rows = COLS - LANES
    for phase in range(PHASES):
        first = LANES - CASES * phase
        windows[:, phase * LANES:(phase + 1) * LANES] = signal_t[first:first + rows, :].astype(BF16)
    parts = [None] * SEG_BLOCKS
    for block in range(1, BLOCKS, 2):
        low = max(SPANS - 1 - block, 0)
        high = min(SPANS + 2 - block, SPANS - 1)
        out = lax.dot_general(
            windows[(block - 1) * LANES:(block + 1) * LANES, :],
            weights[low * hots:(high + 1) * hots, :],
            (((1,), (1,)), ((), ())),
            preferred_element_type=F32,
        )
        for half in range(2):
            for span in range(low, high + 1):
                target = block + half + span - SPANS
                if 0 <= target < SEG_BLOCKS:
                    piece = out[half * LANES:(half + 1) * LANES, (span - low) * hots:(span - low + 1) * hots]
                    parts[target] = piece if parts[target] is None else parts[target] + piece
    return jnp.concatenate(parts, axis=0)


def pack_strains(value, out_ref, scratch):
    half = SEG_COLS // 2
    hots = value.shape[1]
    scratch[:, 0:hots] = value[0:half]
    scratch[:, hots:2 * hots] = value[half:]
    chunks = out_ref.shape[0]
    size = half // chunks
    for chunk in range(chunks):
        out_ref[chunk, 0:size, :] = scratch[chunk * size:(chunk + 1) * size, :]


def unpack_strains(chunks_ref, scratch):
    chunks = chunks_ref.shape[0]
    size = (SEG_COLS // 2) // chunks
    for chunk in range(chunks):
        scratch[chunk * size:(chunk + 1) * size, :] = chunks_ref[chunk, 0:size, :]


def strain_kernel(taps_ref, forces_ref, measured_ref, part_ref, measured_t_ref, signal_t, windows, weights, packed):
    for block in range(BLOCKS):
        cols = slice(block * LANES, (block + 1) * LANES)
        signal_t[cols, :] = forces_ref[:, cols].astype(F32).T
    result = forward_product(signal_t, taps_ref, windows, weights)
    part_ref[...] = jnp.zeros_like(part_ref)
    pack_strains(result, part_ref, packed)
    half = SEG_COLS // 2
    hots = measured_ref.shape[0]
    measured_t = measured_ref[...].T
    measured_t_ref[:, 0:hots] = measured_t[0:half]
    measured_t_ref[:, hots:2 * hots] = measured_t[half:]


def gradient_kernel(core_ref, taps_ref, strains_ref, measured_t_ref, kept_ref, sent_ref, residual_ref, packed, padded, windows, weights, total):
    hots = taps_ref.shape[1]
    half = SEG_COLS // 2
    unpack_strains(strains_ref, packed)
    residual = measured_t_ref[...] - packed[...]
    residual_ref[...] = residual
    padded[...] = jnp.zeros_like(padded)
    for lane, shift in ((0, 0), (hots, CASES)):
        padded[LANES - shift:LANES - shift + half, lane:lane + hots] = residual[:, 0:hots]
        padded[LANES - shift + half:LANES - shift + 2 * half, lane:lane + hots] = residual[:, hots:2 * hots]
    fill_adjoint_weights(taps_ref, weights)
    rows = windows.shape[0]
    for pair in range(PHASES // 2):
        first = 2 * CASES * pair
        windows[:, pair * 2 * hots:(pair + 1) * 2 * hots] = padded[first:first + rows, :].astype(BF16)
    seen = set()
    for span in range(0, SPANS, 2):
        out = jnp.dot(windows[...], weights[:, span * LANES:(span + 2) * LANES], preferred_element_type=F32)
        for side in range(2):
            for row in range(rows // LANES):
                block = row - 1 + SPANS - (span + side)
                piece = out[row * LANES:(row + 1) * LANES, side * LANES:(side + 1) * LANES]
                cols = slice(block * LANES, (block + 1) * LANES)
                if block in seen:
                    total[cols, :] += piece
                else:
                    total[cols, :] = piece
                    seen.add(block)
    rows = kept_ref.shape[0]
    kept_ref[...] = total[pl.ds(pl.multiple_of(core_ref[0] * rows, rows), rows), :]
    sent_ref[...] = total[pl.ds(pl.multiple_of((1 - core_ref[0]) * rows, rows), rows), :]


def join_halves(core_ref, own_ref, other_ref, signal_t):
    rows = own_ref.shape[0]
    signal_t[pl.ds(pl.multiple_of(core_ref[0] * rows, rows), rows), :] = own_ref[...]
    signal_t[pl.ds(pl.multiple_of((1 - core_ref[0]) * rows, rows), rows), :] = other_ref[...]


def image_kernel(core_ref, taps_ref, own_ref, other_ref, part_ref, signal_t, windows, weights, packed):
    join_halves(core_ref, own_ref, other_ref, signal_t)
    result = forward_product(signal_t, taps_ref, windows, weights)
    gradient = signal_t[...]
    squares = jnp.sum(gradient * gradient, axis=0, keepdims=True)
    pack_strains(result, part_ref, packed)
    size = (SEG_COLS // 2) // part_ref.shape[0]
    for chunk in range(part_ref.shape[0]):
        part_ref[chunk, size:, :] = jnp.broadcast_to(squares, (part_ref.shape[1] - size, LANES))


def update_kernel(core_ref, forces_ref, own_ref, other_ref, image_ref, residual_ref, forces_out, residual_out, signal_t, packed):
    size = (SEG_COLS // 2) // image_ref.shape[0]
    squares = image_ref[0, size:size + 1, :]
    image_squares = jnp.zeros((1, LANES), F32)
    for chunk in range(image_ref.shape[0]):
        image_squares = image_squares + image_ref[chunk, size + 1:size + 2, :]
    step_size = jnp.sum(squares, axis=1, keepdims=True) / jnp.sum(image_squares, axis=1, keepdims=True)
    unpack_strains(image_ref, packed)
    left = residual_ref[...] - step_size * packed[...]
    hots = residual_out.shape[0]
    half = SEG_COLS // 2
    left_t = jnp.concatenate([left[:, 0:hots], left[:, hots:2 * hots]], axis=0)
    residual_out[...] = left_t.T
    join_halves(core_ref, own_ref, other_ref, signal_t)
    for block in range(BLOCKS):
        cols = slice(block * LANES, (block + 1) * LANES)
        forces_out[:, cols] = forces_ref[:, cols].astype(F32) + step_size * signal_t[cols, :].T


def call(kernel, outs, scratch, operands):
    spaces = [pltpu.SMEM if operand.dtype == jnp.int32 else pltpu.VMEM for operand in operands]
    return pl.pallas_call(
        kernel,
        out_shape=outs,
        in_specs=[pl.BlockSpec(memory_space=space) for space in spaces],
        scratch_shapes=scratch,
        compiler_params=pltpu.CompilerParams(vmem_limit_bytes=VMEM_LIMIT),
    )(*operands)


def body(response, forces, measured):
    hots, loads, _ = response.shape
    load_axes = ("zl", "y")
    peers = lax.axis_size(load_axes)
    core = lax.axis_index("c").astype(jnp.int32).reshape(1)
    half = SEG_COLS // 2
    rows = half // peers
    chunk_rows = -(-(rows + 2) // 8) * 8
    part = jax.ShapeDtypeStruct((peers, chunk_rows, LANES), F32)
    packed_shape = jax.ShapeDtypeStruct((half, 2 * hots), F32)
    core_shape = jax.ShapeDtypeStruct((COLS // 2, loads), F32)
    forward_scratch = [
        pltpu.VMEM((COLS, loads), F32),
        pltpu.VMEM((COLS - LANES, PHASES * loads), BF16),
        pltpu.VMEM((SPANS * hots, PHASES * loads), BF16),
        pltpu.VMEM((half, 2 * hots), F32),
    ]

    def spread(value, count):
        return jnp.broadcast_to(value[None], (count,) + value.shape)

    def scatter_sum(value, axis):
        return jnp.sum(lax.all_to_all(value, axis, 0, 0), axis=0)

    def gather(value, axis):
        return lax.all_to_all(spread(value, lax.axis_size(axis)), axis, 0, 0)

    def swapped(value, axis, pairs):
        return lax.ppermute(value, axis, pairs + [(b, a) for a, b in pairs])

    taps = jnp.transpose(response, (2, 0, 1))
    strain_part, measured_t = call(
        strain_kernel, (part, packed_shape), forward_scratch, (taps, forces, measured)
    )
    strains = gather(scatter_sum(strain_part, load_axes), load_axes)
    kept, sent, residual = call(
        gradient_kernel,
        (core_shape, core_shape, packed_shape),
        [
            pltpu.VMEM((half, 2 * hots), F32),
            pltpu.VMEM((SEG_COLS + 2 * LANES, 2 * hots), F32),
            pltpu.VMEM((SEG_COLS + LANES, PHASES * hots), BF16),
            pltpu.VMEM((PHASES * hots, SPANS * loads), BF16),
            pltpu.VMEM((COLS, loads), F32),
        ],
        (core, taps, strains, measured_t),
    )
    cores = [(0, 1)]
    own = kept + swapped(sent, "c", cores)
    own = scatter_sum(own.reshape(lax.axis_size("x"), -1, loads), "x")
    own = own + swapped(own, "zh", [(0, 1), (2, 3)])
    own = own + swapped(own, "zh", [(1, 2), (3, 0)])
    own = gather(own, "x").reshape(COLS // 2, loads)
    other = swapped(own, "c", cores)
    image_part = call(image_kernel, part, forward_scratch, (core, taps, own, other))
    image = scatter_sum(image_part, load_axes)
    squares = jnp.sum(image[:rows] * image[:rows], axis=0, keepdims=True)
    squares = squares + swapped(squares, "c", cores)
    squares = jnp.sum(gather(squares, ("zh", "x")), axis=0)
    image = gather(jnp.concatenate([image[:rows + 1], squares, image[rows + 2:]], axis=0), load_axes)
    return call(
        update_kernel,
        (jax.ShapeDtypeStruct((loads, COLS), F32), jax.ShapeDtypeStruct((hots, SEG_COLS), F32)),
        [pltpu.VMEM((COLS, loads), F32), pltpu.VMEM((half, 2 * hots), F32)],
        (core, forces, own, other, image, residual),
    )


def solution(mesh):
    parts = Mesh(mesh.devices.reshape(4, 4, 2, 4, 4), ("zh", "x", "c", "zl", "y"))
    hot, load = ("zh", "x", "c"), ("zl", "y")
    return jax.shard_map(
        body,
        mesh=parts,
        in_specs=(P(hot, load, None), P(load, None), P(hot, None)),
        out_specs=(P(load, None), P(hot, None)),
        check_vma=False,
    )
```

```python
import jax
import jax.numpy as jnp
from jax import lax
from jax.experimental import pallas as pl
from jax.experimental.pallas import tpu as pltpu
from jax.sharding import Mesh, PartitionSpec as P

TAPS = 128
SEG = 48
CASES = 8
HIST = 128
STEPS = 176
LANES = 128
PHASES = LANES // CASES
SPANS = TAPS // PHASES
SEG_COLS = SEG * CASES
SEG_BLOCKS = SEG_COLS // LANES
COLS = STEPS * CASES
GROUP = 4
BLOCKS = COLS // LANES
F32 = jnp.float32
BF16 = jnp.bfloat16
VMEM_LIMIT = 40 * 1024 * 1024


def forward_product(signal_t, taps_ref):
    hots = taps_ref.shape[1]
    parts = [None] * SEG_BLOCKS
    for block in range(1, BLOCKS, 2):
        low = max(SPANS - 1 - block, 0)
        high = min(SPANS + 2 - block, SPANS - 1)
        first = block * LANES
        windows = [signal_t[first - CASES * phase:first - CASES * phase + 2 * LANES, :].astype(BF16) for phase in range(PHASES)]
        weights = [
            jnp.concatenate([taps_ref[span * PHASES + phase] for phase in range(PHASES)], axis=1)
            for span in range(low, high + 1)
        ]
        out = lax.dot_general(
            jnp.concatenate(windows, axis=1),
            jnp.concatenate(weights, axis=0),
            (((1,), (1,)), ((), ())),
            preferred_element_type=F32,
        )
        for half in range(2):
            for span in range(low, high + 1):
                target = block + half + span - SPANS
                if 0 <= target < SEG_BLOCKS:
                    piece = out[half * LANES:(half + 1) * LANES, (span - low) * hots:(span - low + 1) * hots]
                    parts[target] = piece if parts[target] is None else parts[target] + piece
    return jnp.concatenate(parts, axis=0)


def pack_strains(value, out_ref, scratch):
    half = SEG_COLS // 2
    hots = value.shape[1]
    scratch[:, 0:hots] = value[0:half]
    scratch[:, hots:2 * hots] = value[half:]
    groups = out_ref.shape[1]
    for group in range(half // GROUP):
        out_ref[group // groups, group % groups] = scratch[group * GROUP:(group + 1) * GROUP, :]


def unpack_strains(chunks_ref, scratch):
    half = SEG_COLS // 2
    groups = half // GROUP // chunks_ref.shape[0]
    for group in range(half // GROUP):
        scratch[group * GROUP:(group + 1) * GROUP, :] = chunks_ref[group // groups, group % groups]


def strain_kernel(taps_ref, forces_ref, measured_ref, part_ref, measured_t_ref, signal_t, packed):
    for block in range(BLOCKS):
        cols = slice(block * LANES, (block + 1) * LANES)
        signal_t[cols, :] = forces_ref[:, cols].astype(F32).T
    result = forward_product(signal_t, taps_ref)
    pack_strains(result, part_ref, packed)
    half = SEG_COLS // 2
    hots = measured_ref.shape[0]
    measured_t = measured_ref[...].T
    measured_t_ref[:, 0:hots] = measured_t[0:half]
    measured_t_ref[:, hots:2 * hots] = measured_t[half:]


def gradient_kernel(core_ref, taps_ref, strains_ref, measured_t_ref, kept_ref, sent_ref, residual_ref, packed, padded, windows, total):
    hots = taps_ref.shape[1]
    half = SEG_COLS // 2
    unpack_strains(strains_ref, packed)
    residual = measured_t_ref[...] - packed[...]
    residual_ref[...] = residual
    padded[...] = jnp.zeros_like(padded)
    for lane, shift in ((0, 0), (hots, CASES)):
        padded[LANES - shift:LANES - shift + half, lane:lane + hots] = residual[:, 0:hots]
        padded[LANES - shift + half:LANES - shift + 2 * half, lane:lane + hots] = residual[:, hots:2 * hots]
    rows = windows.shape[0]
    for pair in range(PHASES // 2):
        first = 2 * CASES * pair
        windows[:, pair * 2 * hots:(pair + 1) * 2 * hots] = padded[first:first + rows, :].astype(BF16)
    seen = set()
    for span in range(0, SPANS, 2):
        weights = [
            jnp.concatenate([taps_ref[span * PHASES + phase], taps_ref[(span + 1) * PHASES + phase]], axis=1)
            for phase in range(PHASES)
        ]
        out = jnp.dot(windows[...], jnp.concatenate(weights, axis=0), preferred_element_type=F32)
        for side in range(2):
            for row in range(rows // LANES):
                block = row - 1 + SPANS - (span + side)
                piece = out[row * LANES:(row + 1) * LANES, side * LANES:(side + 1) * LANES]
                cols = slice(block * LANES, (block + 1) * LANES)
                if block in seen:
                    total[cols, :] += piece
                else:
                    total[cols, :] = piece
                    seen.add(block)
    rows = kept_ref.shape[0]
    kept_ref[...] = total[pl.ds(pl.multiple_of(core_ref[0] * rows, rows), rows), :]
    sent_ref[...] = total[pl.ds(pl.multiple_of((1 - core_ref[0]) * rows, rows), rows), :]


def join_halves(core_ref, own_ref, other_ref, signal_t):
    rows = own_ref.shape[0]
    signal_t[pl.ds(pl.multiple_of(core_ref[0] * rows, rows), rows), :] = own_ref[...]
    signal_t[pl.ds(pl.multiple_of((1 - core_ref[0]) * rows, rows), rows), :] = other_ref[...]


def image_kernel(core_ref, taps_ref, own_ref, other_ref, part_ref, squares_ref, signal_t, packed):
    join_halves(core_ref, own_ref, other_ref, signal_t)
    result = forward_product(signal_t, taps_ref)
    gradient = signal_t[...]
    squares_ref[...] = jnp.sum(gradient * gradient, axis=0, keepdims=True)
    pack_strains(result, part_ref, packed)


def turn_kernel(core_ref, own_ref, other_ref, out_ref, signal_t):
    join_halves(core_ref, own_ref, other_ref, signal_t)
    for block in range(BLOCKS):
        cols = slice(block * LANES, (block + 1) * LANES)
        out_ref[:, cols] = signal_t[cols, :].T


def update_kernel(forces_ref, gradient_ref, image_ref, residual_ref, forces_out, residual_out, packed):
    squares = image_ref[0, image_ref.shape[1] - 1]
    for chunk in range(1, image_ref.shape[0]):
        squares = squares + image_ref[chunk, image_ref.shape[1] - 1]
    squares = jnp.sum(squares, axis=1, keepdims=True)
    step_size = squares[1:2] / squares[0:1]
    unpack_strains(image_ref, packed)
    left = residual_ref[...] - step_size * packed[...]
    hots = residual_out.shape[0]
    left_t = jnp.concatenate([left[:, 0:hots], left[:, hots:2 * hots]], axis=0)
    residual_out[...] = left_t.T
    forces_out[...] = forces_ref[...].astype(F32) + step_size * gradient_ref[...]


def call(kernel, outs, scratch, operands):
    spaces = [pltpu.SMEM if operand.dtype == jnp.int32 else pltpu.VMEM for operand in operands]
    return pl.pallas_call(
        kernel,
        out_shape=outs,
        in_specs=[pl.BlockSpec(memory_space=space) for space in spaces],
        scratch_shapes=scratch,
        compiler_params=pltpu.CompilerParams(vmem_limit_bytes=VMEM_LIMIT),
    )(*operands)


def body(response, forces, measured):
    hots, loads, _ = response.shape
    load_axes = ("zl", "y")
    peers = lax.axis_size(load_axes)
    core = lax.axis_index("c").astype(jnp.int32).reshape(1)
    half = SEG_COLS // 2
    part = jax.ShapeDtypeStruct((peers, half // peers // GROUP, GROUP, LANES), F32)
    packed_shape = jax.ShapeDtypeStruct((half, 2 * hots), F32)
    core_shape = jax.ShapeDtypeStruct((COLS // 2, loads), F32)
    forward_scratch = [
        pltpu.VMEM((COLS, loads), F32),
        pltpu.VMEM((half, 2 * hots), F32),
    ]

    def spread(value, count):
        return jnp.broadcast_to(value[None], (count,) + value.shape)

    def scatter_sum(value, axis):
        return jnp.sum(lax.all_to_all(value, axis, 0, 0), axis=0)

    def gather(value, axis):
        return lax.all_to_all(spread(value, lax.axis_size(axis)), axis, 0, 0)

    def swapped(value, axis, pairs):
        return lax.ppermute(value, axis, pairs + [(b, a) for a, b in pairs])

    taps, core = lax.optimization_barrier((jnp.transpose(response, (2, 0, 1)), core))
    strain_part, measured_t = call(
        strain_kernel, (part, packed_shape), forward_scratch, (taps, forces, measured)
    )
    strains = gather(scatter_sum(strain_part, load_axes), load_axes)
    kept, sent, residual = call(
        gradient_kernel,
        (core_shape, core_shape, packed_shape),
        [
            pltpu.VMEM((half, 2 * hots), F32),
            pltpu.VMEM((SEG_COLS + 2 * LANES, 2 * hots), F32),
            pltpu.VMEM((SEG_COLS + LANES, PHASES * hots), BF16),
            pltpu.VMEM((COLS, loads), F32),
        ],
        (core, taps, strains, measured_t),
    )
    cores = [(0, 1)]
    own = kept + swapped(sent, "c", cores)
    own = scatter_sum(own.reshape(lax.axis_size("x"), -1, loads), "x")
    inner, outer = [(0, 1), (2, 3)], [(1, 2), (3, 0)]
    for even, odd in ((inner, outer), (outer, inner)):
        pairs = [(2 * i, 2 * j) for i, j in even] + [(2 * i + 1, 2 * j + 1) for i, j in odd]
        own = own + swapped(own, ("zh", "c"), pairs)
    own = gather(own, "x").reshape(COLS // 2, loads)
    other = swapped(own, "c", cores)
    image_part, own_squares = call(
        image_kernel, (part, jax.ShapeDtypeStruct((1, loads), F32)), forward_scratch, (core, taps, own, other)
    )
    image = scatter_sum(image_part, load_axes)
    squares = jnp.sum(image * image, axis=(0, 1))[None]
    others = swapped(squares, "c", cores)
    halves = lax.optimization_barrier((own, other, squares))[:2]
    gradient = call(
        turn_kernel,
        jax.ShapeDtypeStruct((loads, COLS), F32),
        [pltpu.VMEM((COLS, loads), F32)],
        (core,) + halves,
    )
    squares, gradient = lax.optimization_barrier((squares + others, gradient))
    squares = jnp.sum(gather(squares, ("zh", "x")), axis=0)
    image, squares, own_squares = lax.optimization_barrier((image, squares, own_squares))
    extra = jnp.concatenate([squares, own_squares] * (GROUP // 2), axis=0)
    image = gather(jnp.concatenate([image, extra[None]], axis=0), load_axes)
    return call(
        update_kernel,
        (jax.ShapeDtypeStruct((loads, COLS), F32), jax.ShapeDtypeStruct((hots, SEG_COLS), F32)),
        [pltpu.VMEM((half, 2 * hots), F32)],
        (forces, gradient, image, residual),
    )


def solution(mesh):
    parts = Mesh(mesh.devices.reshape(4, 4, 2, 4, 4), ("zh", "x", "c", "zl", "y"))
    hot, load = ("zh", "x", "c"), ("zl", "y")
    return jax.shard_map(
        body,
        mesh=parts,
        in_specs=(P(hot, load, None), P(load, None), P(hot, None)),
        out_specs=(P(load, None), P(hot, None)),
        check_vma=False,
    )
```

```python
import jax
import jax.numpy as jnp
from jax import lax
from jax.experimental import pallas as pl
from jax.experimental.pallas import tpu as pltpu
from jax.sharding import Mesh, PartitionSpec as P

TAPS = 128
SEG = 48
CASES = 8
HIST = 128
STEPS = 176
LANES = 128
PHASES = LANES // CASES
SPANS = TAPS // PHASES
SEG_COLS = SEG * CASES
SEG_BLOCKS = SEG_COLS // LANES
COLS = STEPS * CASES
GROUP = 4
BLOCKS = COLS // LANES
F32 = jnp.float32
BF16 = jnp.bfloat16
VMEM_LIMIT = 40 * 1024 * 1024


def forward_product(signal_t, taps_ref):
    hots = taps_ref.shape[1]
    parts = [None] * SEG_BLOCKS
    for block in range(1, BLOCKS, 2):
        low = max(SPANS - 1 - block, 0)
        high = min(SPANS + 2 - block, SPANS - 1)
        first = block * LANES
        windows = [signal_t[first - CASES * phase:first - CASES * phase + 2 * LANES, :].astype(BF16) for phase in range(PHASES)]
        weights = [
            jnp.concatenate([taps_ref[span * PHASES + phase] for phase in range(PHASES)], axis=1)
            for span in range(low, high + 1)
        ]
        out = lax.dot_general(
            jnp.concatenate(windows, axis=1),
            jnp.concatenate(weights, axis=0),
            (((1,), (1,)), ((), ())),
            preferred_element_type=F32,
        )
        for half in range(2):
            for span in range(low, high + 1):
                target = block + half + span - SPANS
                if 0 <= target < SEG_BLOCKS:
                    piece = out[half * LANES:(half + 1) * LANES, (span - low) * hots:(span - low + 1) * hots]
                    parts[target] = piece if parts[target] is None else parts[target] + piece
    return jnp.concatenate(parts, axis=0)


def pack_strains(value, out_ref, scratch):
    half = SEG_COLS // 2
    hots = value.shape[1]
    scratch[:, 0:hots] = value[0:half]
    scratch[:, hots:2 * hots] = value[half:]
    groups = out_ref.shape[1]
    for group in range(half // GROUP):
        out_ref[group // groups, group % groups] = scratch[group * GROUP:(group + 1) * GROUP, :]


def unpack_strains(chunks_ref, scratch):
    half = SEG_COLS // 2
    groups = half // GROUP // chunks_ref.shape[0]
    for group in range(half // GROUP):
        scratch[group * GROUP:(group + 1) * GROUP, :] = chunks_ref[group // groups, group % groups]


def strain_kernel(taps_ref, forces_ref, measured_ref, part_ref, measured_t_ref, signal_t, packed):
    for block in range(BLOCKS):
        cols = slice(block * LANES, (block + 1) * LANES)
        signal_t[cols, :] = forces_ref[:, cols].astype(F32).T
    result = forward_product(signal_t, taps_ref)
    pack_strains(result, part_ref, packed)
    half = SEG_COLS // 2
    hots = measured_ref.shape[0]
    measured_t = measured_ref[...].T
    measured_t_ref[:, 0:hots] = measured_t[0:half]
    measured_t_ref[:, hots:2 * hots] = measured_t[half:]


def gradient_kernel(taps_ref, strains_ref, measured_t_ref, part_ref, residual_ref, packed, padded, windows):
    hots = taps_ref.shape[1]
    half = SEG_COLS // 2
    unpack_strains(strains_ref, packed)
    residual = measured_t_ref[...] - packed[...]
    residual_ref[...] = residual
    padded[...] = jnp.zeros_like(padded)
    for lane, shift in ((0, 0), (hots, CASES)):
        padded[LANES - shift:LANES - shift + half, lane:lane + hots] = residual[:, 0:hots]
        padded[LANES - shift + half:LANES - shift + 2 * half, lane:lane + hots] = residual[:, hots:2 * hots]
    rows = windows.shape[0]
    for pair in range(PHASES // 2):
        first = 2 * CASES * pair
        windows[:, pair * 2 * hots:(pair + 1) * 2 * hots] = padded[first:first + rows, :].astype(BF16)
    seen = set()
    for span in range(0, SPANS, 2):
        weights = [
            jnp.concatenate([taps_ref[span * PHASES + phase], taps_ref[(span + 1) * PHASES + phase]], axis=1)
            for phase in range(PHASES)
        ]
        out = jnp.dot(windows[...], jnp.concatenate(weights, axis=0), preferred_element_type=F32)
        for side in range(2):
            for row in range(rows // LANES):
                block = row - 1 + SPANS - (span + side)
                piece = out[row * LANES:(row + 1) * LANES, side * LANES:(side + 1) * LANES]
                cols = slice(block * LANES, (block + 1) * LANES)
                if block in seen:
                    part_ref[cols, :] += piece
                else:
                    part_ref[cols, :] = piece
                    seen.add(block)


def join_halves(core_ref, own_ref, other_ref, signal_t):
    rows = own_ref.shape[0]
    signal_t[pl.ds(pl.multiple_of(core_ref[0] * rows, rows), rows), :] = own_ref[...]
    signal_t[pl.ds(pl.multiple_of((1 - core_ref[0]) * rows, rows), rows), :] = other_ref[...]


def image_kernel(core_ref, taps_ref, own_ref, other_ref, part_ref, squares_ref, signal_t, packed):
    join_halves(core_ref, own_ref, other_ref, signal_t)
    result = forward_product(signal_t, taps_ref)
    gradient = signal_t[...]
    squares_ref[...] = jnp.sum(gradient * gradient, axis=0, keepdims=True)
    pack_strains(result, part_ref, packed)


def update_kernel(core_ref, forces_ref, own_ref, other_ref, image_ref, residual_ref, forces_out, residual_out, signal_t, packed):
    squares = image_ref[0, image_ref.shape[1] - 1]
    for chunk in range(1, image_ref.shape[0]):
        squares = squares + image_ref[chunk, image_ref.shape[1] - 1]
    squares = jnp.sum(squares, axis=1, keepdims=True)
    step_size = squares[1:2] / squares[0:1]
    unpack_strains(image_ref, packed)
    left = residual_ref[...] - step_size * packed[...]
    hots = residual_out.shape[0]
    left_t = jnp.concatenate([left[:, 0:hots], left[:, hots:2 * hots]], axis=0)
    residual_out[...] = left_t.T
    join_halves(core_ref, own_ref, other_ref, signal_t)
    for block in range(BLOCKS):
        cols = slice(block * LANES, (block + 1) * LANES)
        forces_out[:, cols] = forces_ref[:, cols].astype(F32) + step_size * signal_t[cols, :].T


def call(kernel, outs, scratch, operands):
    spaces = [pltpu.SMEM if operand.dtype == jnp.int32 else pltpu.VMEM for operand in operands]
    return pl.pallas_call(
        kernel,
        out_shape=outs,
        in_specs=[pl.BlockSpec(memory_space=space) for space in spaces],
        scratch_shapes=scratch,
        compiler_params=pltpu.CompilerParams(vmem_limit_bytes=VMEM_LIMIT),
    )(*operands)


def body(response, forces, measured):
    hots, loads, _ = response.shape
    load_axes = ("zl", "y")
    peers = lax.axis_size(load_axes)
    core = lax.axis_index("c").astype(jnp.int32).reshape(1)
    half = SEG_COLS // 2
    part = jax.ShapeDtypeStruct((peers, half // peers // GROUP, GROUP, LANES), F32)
    packed_shape = jax.ShapeDtypeStruct((half, 2 * hots), F32)
    forward_scratch = [
        pltpu.VMEM((COLS, loads), F32),
        pltpu.VMEM((half, 2 * hots), F32),
    ]

    def spread(value, count):
        return jnp.broadcast_to(value[None], (count,) + value.shape)

    def scatter_sum(value, axis):
        return jnp.sum(lax.all_to_all(value, axis, 0, 0), axis=0)

    def gather(value, axis):
        return lax.all_to_all(spread(value, lax.axis_size(axis)), axis, 0, 0)

    def swapped(value, axis, pairs):
        return lax.ppermute(value, axis, pairs + [(b, a) for a, b in pairs])

    taps, core = lax.optimization_barrier((jnp.transpose(response, (2, 0, 1)), core))
    strain_part, measured_t = call(
        strain_kernel, (part, packed_shape), forward_scratch, (taps, forces, measured)
    )
    strains = gather(scatter_sum(strain_part, load_axes), load_axes)
    gradient_part, residual = call(
        gradient_kernel,
        (jax.ShapeDtypeStruct((COLS, loads), F32), packed_shape),
        [
            pltpu.VMEM((half, 2 * hots), F32),
            pltpu.VMEM((SEG_COLS + 2 * LANES, 2 * hots), F32),
            pltpu.VMEM((SEG_COLS + LANES, PHASES * hots), BF16),
        ],
        (taps, strains, measured_t),
    )
    cores = [(0, 1)]
    near = ("c", "x")
    own = scatter_sum(gradient_part.reshape(lax.axis_size(near), -1, loads), near)
    inner, outer = [(0, 1), (2, 3)], [(1, 2), (3, 0)]
    for even, odd in ((inner, outer), (outer, inner)):
        pairs = [(2 * i, 2 * j) for i, j in even] + [(2 * i + 1, 2 * j + 1) for i, j in odd]
        own = own + swapped(own, ("zh", "c"), pairs)
    own = gather(own, "x").reshape(COLS // 2, loads)
    other = swapped(own, "c", cores)
    image_part, own_squares = call(
        image_kernel, (part, jax.ShapeDtypeStruct((1, loads), F32)), forward_scratch, (core, taps, own, other)
    )
    image = scatter_sum(image_part, load_axes)
    squares = jnp.sum(image * image, axis=(0, 1))[None]
    squares = jnp.sum(gather(squares, ("zh", "x", "c")), axis=0)
    image, squares, own_squares = lax.optimization_barrier((image, squares, own_squares))
    extra = jnp.concatenate([squares, own_squares] * (GROUP // 2), axis=0)
    image = gather(jnp.concatenate([image, extra[None]], axis=0), load_axes)
    return call(
        update_kernel,
        (jax.ShapeDtypeStruct((loads, COLS), F32), jax.ShapeDtypeStruct((hots, SEG_COLS), F32)),
        [pltpu.VMEM((COLS, loads), F32), pltpu.VMEM((half, 2 * hots), F32)],
        (core, forces, own, other, image, residual),
    )


def solution(mesh):
    parts = Mesh(mesh.devices.reshape(4, 4, 2, 4, 4), ("zh", "x", "c", "zl", "y"))
    hot, load = ("zh", "x", "c"), ("zl", "y")
    return jax.shard_map(
        body,
        mesh=parts,
        in_specs=(P(hot, load, None), P(load, None), P(hot, None)),
        out_specs=(P(load, None), P(hot, None)),
        check_vma=False,
    )
```

```python
import jax
import jax.numpy as jnp
from jax import lax
from jax.experimental import pallas as pl
from jax.experimental.pallas import tpu as pltpu
from jax.sharding import Mesh, PartitionSpec as P

TAPS = 128
SEG = 48
CASES = 8
HIST = 128
STEPS = 176
LANES = 128
PHASES = LANES // CASES
SPANS = TAPS // PHASES
SEG_COLS = SEG * CASES
SEG_BLOCKS = SEG_COLS // LANES
COLS = STEPS * CASES
GROUP = 4
BLOCKS = COLS // LANES
F32 = jnp.float32
BF16 = jnp.bfloat16
VMEM_LIMIT = 40 * 1024 * 1024


def forward_product(signal_t, taps_ref):
    hots = taps_ref.shape[1]
    parts = [None] * SEG_BLOCKS
    for block in range(1, BLOCKS, 2):
        low = max(SPANS - 1 - block, 0)
        high = min(SPANS + 2 - block, SPANS - 1)
        first = block * LANES
        windows = [signal_t[first - CASES * phase:first - CASES * phase + 2 * LANES, :].astype(BF16) for phase in range(PHASES)]
        weights = [
            jnp.concatenate([taps_ref[span * PHASES + phase] for phase in range(PHASES)], axis=1)
            for span in range(low, high + 1)
        ]
        out = lax.dot_general(
            jnp.concatenate(windows, axis=1),
            jnp.concatenate(weights, axis=0),
            (((1,), (1,)), ((), ())),
            preferred_element_type=F32,
        )
        for half in range(2):
            for span in range(low, high + 1):
                target = block + half + span - SPANS
                if 0 <= target < SEG_BLOCKS:
                    piece = out[half * LANES:(half + 1) * LANES, (span - low) * hots:(span - low + 1) * hots]
                    parts[target] = piece if parts[target] is None else parts[target] + piece
    return jnp.concatenate(parts, axis=0)


def pack_strains(value, out_ref, scratch):
    half = SEG_COLS // 2
    hots = value.shape[1]
    scratch[:, 0:hots] = value[0:half]
    scratch[:, hots:2 * hots] = value[half:]
    groups = out_ref.shape[1]
    for group in range(half // GROUP):
        out_ref[group // groups, group % groups] = scratch[group * GROUP:(group + 1) * GROUP, :]


def unpack_strains(chunks_ref, scratch):
    half = SEG_COLS // 2
    groups = half // GROUP // chunks_ref.shape[0]
    for group in range(half // GROUP):
        scratch[group * GROUP:(group + 1) * GROUP, :] = chunks_ref[group // groups, group % groups]


def strain_kernel(taps_ref, forces_ref, measured_ref, part_ref, measured_t_ref, signal_t, packed):
    for block in range(BLOCKS):
        cols = slice(block * LANES, (block + 1) * LANES)
        signal_t[cols, :] = forces_ref[:, cols].astype(F32).T
    result = forward_product(signal_t, taps_ref)
    pack_strains(result, part_ref, packed)
    half = SEG_COLS // 2
    hots = measured_ref.shape[0]
    measured_t = measured_ref[...].T
    measured_t_ref[:, 0:hots] = measured_t[0:half]
    measured_t_ref[:, hots:2 * hots] = measured_t[half:]


def gradient_kernel(taps_ref, strains_ref, measured_t_ref, part_ref, residual_ref, packed, padded, windows):
    hots = taps_ref.shape[1]
    half = SEG_COLS // 2
    unpack_strains(strains_ref, packed)
    residual = measured_t_ref[...] - packed[...]
    residual_ref[...] = residual
    padded[...] = jnp.zeros_like(padded)
    for lane, shift in ((0, 0), (hots, CASES)):
        padded[LANES - shift:LANES - shift + half, lane:lane + hots] = residual[:, 0:hots]
        padded[LANES - shift + half:LANES - shift + 2 * half, lane:lane + hots] = residual[:, hots:2 * hots]
    rows = windows.shape[0]
    for pair in range(PHASES // 2):
        first = 2 * CASES * pair
        windows[:, pair * 2 * hots:(pair + 1) * 2 * hots] = padded[first:first + rows, :].astype(BF16)
    seen = set()
    for span in range(0, SPANS, 2):
        weights = [
            jnp.concatenate([taps_ref[span * PHASES + phase], taps_ref[(span + 1) * PHASES + phase]], axis=1)
            for phase in range(PHASES)
        ]
        out = jnp.dot(windows[...], jnp.concatenate(weights, axis=0), preferred_element_type=F32)
        for side in range(2):
            for row in range(rows // LANES):
                block = row - 1 + SPANS - (span + side)
                piece = out[row * LANES:(row + 1) * LANES, side * LANES:(side + 1) * LANES]
                cols = slice(block * LANES, (block + 1) * LANES)
                if block in seen:
                    part_ref[cols, :] += piece
                else:
                    part_ref[cols, :] = piece
                    seen.add(block)


def join_halves(core_ref, own_ref, other_ref, signal_t):
    rows = own_ref.shape[0]
    signal_t[pl.ds(pl.multiple_of(core_ref[0] * rows, rows), rows), :] = own_ref[...]
    signal_t[pl.ds(pl.multiple_of((1 - core_ref[0]) * rows, rows), rows), :] = other_ref[...]


def image_kernel(core_ref, taps_ref, own_ref, other_ref, part_ref, squares_ref, signal_t, packed):
    join_halves(core_ref, own_ref, other_ref, signal_t)
    result = forward_product(signal_t, taps_ref)
    gradient = signal_t[...]
    squares_ref[...] = jnp.sum(gradient * gradient, axis=0, keepdims=True)
    pack_strains(result, part_ref, packed)


def update_kernel(core_ref, forces_ref, own_ref, other_ref, image_ref, residual_ref, forces_out, residual_out, signal_t, packed):
    squares = image_ref[0, image_ref.shape[1] - 1]
    for chunk in range(1, image_ref.shape[0]):
        squares = squares + image_ref[chunk, image_ref.shape[1] - 1]
    squares = jnp.sum(squares, axis=1, keepdims=True)
    step_size = squares[1:2] / squares[0:1]
    unpack_strains(image_ref, packed)
    left = residual_ref[...] - step_size * packed[...]
    hots = residual_out.shape[0]
    left_t = jnp.concatenate([left[:, 0:hots], left[:, hots:2 * hots]], axis=0)
    residual_out[...] = left_t.T
    join_halves(core_ref, own_ref, other_ref, signal_t)
    for block in range(BLOCKS):
        cols = slice(block * LANES, (block + 1) * LANES)
        forces_out[:, cols] = forces_ref[:, cols].astype(F32) + step_size * signal_t[cols, :].T


def call(kernel, outs, scratch, operands):
    spaces = [pltpu.SMEM if operand.dtype == jnp.int32 else pltpu.VMEM for operand in operands]
    return pl.pallas_call(
        kernel,
        out_shape=outs,
        in_specs=[pl.BlockSpec(memory_space=space) for space in spaces],
        scratch_shapes=scratch,
        compiler_params=pltpu.CompilerParams(vmem_limit_bytes=VMEM_LIMIT),
    )(*operands)


def body(response, forces, measured):
    hots, loads, _ = response.shape
    load_axes = ("y", "zl")
    peers = lax.axis_size(load_axes)
    core = lax.axis_index("c").astype(jnp.int32).reshape(1)
    half = SEG_COLS // 2
    part = jax.ShapeDtypeStruct((peers, half // peers // GROUP, GROUP, LANES), F32)
    packed_shape = jax.ShapeDtypeStruct((half, 2 * hots), F32)
    forward_scratch = [
        pltpu.VMEM((COLS, loads), F32),
        pltpu.VMEM((half, 2 * hots), F32),
    ]

    def spread(value, count):
        return jnp.broadcast_to(value[None], (count,) + value.shape)

    def scatter_sum(value, axis):
        return jnp.sum(lax.all_to_all(value, axis, 0, 0), axis=0)

    def gather(value, axis):
        return lax.all_to_all(spread(value, lax.axis_size(axis)), axis, 0, 0)

    def swapped(value, axis, pairs):
        return lax.ppermute(value, axis, pairs + [(b, a) for a, b in pairs])

    taps, core = lax.optimization_barrier((jnp.transpose(response, (2, 0, 1)), core))
    strain_part, measured_t = call(
        strain_kernel, (part, packed_shape), forward_scratch, (taps, forces, measured)
    )
    strains = gather(scatter_sum(strain_part, load_axes), load_axes)
    gradient_part, residual = call(
        gradient_kernel,
        (jax.ShapeDtypeStruct((COLS, loads), F32), packed_shape),
        [
            pltpu.VMEM((half, 2 * hots), F32),
            pltpu.VMEM((SEG_COLS + 2 * LANES, 2 * hots), F32),
            pltpu.VMEM((SEG_COLS + LANES, PHASES * hots), BF16),
        ],
        (taps, strains, measured_t),
    )
    cores = [(0, 1)]
    near = ("c", "x")
    own = scatter_sum(gradient_part.reshape(lax.axis_size(near), -1, loads), near)
    inner, outer = [(0, 1), (2, 3)], [(1, 2), (3, 0)]
    for even, odd in ((inner, outer), (outer, inner)):
        pairs = [(2 * i, 2 * j) for i, j in even] + [(2 * i + 1, 2 * j + 1) for i, j in odd]
        own = own + swapped(own, ("zh", "c"), pairs)
    own = gather(own, "x").reshape(COLS // 2, loads)
    other = swapped(own, "c", cores)
    image_part, own_squares = call(
        image_kernel, (part, jax.ShapeDtypeStruct((1, loads), F32)), forward_scratch, (core, taps, own, other)
    )
    image = scatter_sum(image_part, load_axes)
    squares = jnp.sum(image * image, axis=(0, 1))[None]
    squares = jnp.sum(gather(squares, ("zh", "x", "c")), axis=0)
    image, squares, own_squares = lax.optimization_barrier((image, squares, own_squares))
    extra = jnp.concatenate([squares, own_squares] * (GROUP // 2), axis=0)
    image = gather(jnp.concatenate([image, extra[None]], axis=0), load_axes)
    return call(
        update_kernel,
        (jax.ShapeDtypeStruct((loads, COLS), F32), jax.ShapeDtypeStruct((hots, SEG_COLS), F32)),
        [pltpu.VMEM((COLS, loads), F32), pltpu.VMEM((half, 2 * hots), F32)],
        (core, forces, own, other, image, residual),
    )


def solution(mesh):
    parts = Mesh(mesh.devices.reshape(4, 4, 2, 4, 4), ("zh", "x", "c", "zl", "y"))
    hot, load = ("zh", "x", "c"), ("zl", "y")
    return jax.shard_map(
        body,
        mesh=parts,
        in_specs=(P(hot, load, None), P(load, None), P(hot, None)),
        out_specs=(P(load, None), P(hot, None)),
        check_vma=False,
    )
```

```python
import jax
import jax.numpy as jnp
from jax import lax
from jax.experimental import pallas as pl
from jax.experimental.pallas import tpu as pltpu
from jax.sharding import Mesh, PartitionSpec as P

TAPS = 128
SEG = 48
CASES = 8
HIST = 128
STEPS = 176
LANES = 128
PHASES = LANES // CASES
SPANS = TAPS // PHASES
SEG_COLS = SEG * CASES
SEG_BLOCKS = SEG_COLS // LANES
COLS = STEPS * CASES
GROUP = 4
BLOCKS = COLS // LANES
F32 = jnp.float32
BF16 = jnp.bfloat16
VMEM_LIMIT = 40 * 1024 * 1024


def forward_product(signal_t, taps_ref):
    hots = taps_ref.shape[1]
    parts = [None] * SEG_BLOCKS
    for block in range(1, BLOCKS, 2):
        low = max(SPANS - 1 - block, 0)
        high = min(SPANS + 2 - block, SPANS - 1)
        first = block * LANES
        windows = [signal_t[first - CASES * phase:first - CASES * phase + 2 * LANES, :].astype(BF16) for phase in range(PHASES)]
        weights = [
            jnp.concatenate([taps_ref[span * PHASES + phase] for phase in range(PHASES)], axis=1)
            for span in range(low, high + 1)
        ]
        out = lax.dot_general(
            jnp.concatenate(windows, axis=1),
            jnp.concatenate(weights, axis=0),
            (((1,), (1,)), ((), ())),
            preferred_element_type=F32,
        )
        for half in range(2):
            for span in range(low, high + 1):
                target = block + half + span - SPANS
                if 0 <= target < SEG_BLOCKS:
                    piece = out[half * LANES:(half + 1) * LANES, (span - low) * hots:(span - low + 1) * hots]
                    parts[target] = piece if parts[target] is None else parts[target] + piece
    return jnp.concatenate(parts, axis=0)


def pack_strains(value, out_ref, scratch):
    half = SEG_COLS // 2
    hots = value.shape[1]
    scratch[:, 0:hots] = value[0:half]
    scratch[:, hots:2 * hots] = value[half:]
    groups = out_ref.shape[1]
    for group in range(half // GROUP):
        out_ref[group // groups, group % groups] = scratch[group * GROUP:(group + 1) * GROUP, :]


def unpack_strains(chunks_ref, scratch):
    half = SEG_COLS // 2
    groups = half // GROUP // chunks_ref.shape[0]
    for group in range(half // GROUP):
        scratch[group * GROUP:(group + 1) * GROUP, :] = chunks_ref[group // groups, group % groups]


def strain_kernel(taps_ref, forces_ref, measured_ref, part_ref, measured_t_ref, signal_t, packed):
    for block in range(BLOCKS):
        cols = slice(block * LANES, (block + 1) * LANES)
        signal_t[cols, :] = forces_ref[:, cols].astype(F32).T
    result = forward_product(signal_t, taps_ref)
    pack_strains(result, part_ref, packed)
    half = SEG_COLS // 2
    hots = measured_ref.shape[0]
    measured_t = measured_ref[...].T
    measured_t_ref[:, 0:hots] = measured_t[0:half]
    measured_t_ref[:, hots:2 * hots] = measured_t[half:]


def gradient_kernel(core_ref, taps_ref, strains_ref, measured_t_ref, kept_ref, sent_ref, residual_ref, packed, padded, windows, total):
    hots = taps_ref.shape[1]
    half = SEG_COLS // 2
    unpack_strains(strains_ref, packed)
    residual = measured_t_ref[...] - packed[...]
    residual_ref[...] = residual
    padded[...] = jnp.zeros_like(padded)
    for lane, shift in ((0, 0), (hots, CASES)):
        padded[LANES - shift:LANES - shift + half, lane:lane + hots] = residual[:, 0:hots]
        padded[LANES - shift + half:LANES - shift + 2 * half, lane:lane + hots] = residual[:, hots:2 * hots]
    rows = windows.shape[0]
    for pair in range(PHASES // 2):
        first = 2 * CASES * pair
        windows[:, pair * 2 * hots:(pair + 1) * 2 * hots] = padded[first:first + rows, :].astype(BF16)
    seen = set()
    for span in range(0, SPANS, 2):
        weights = [
            jnp.concatenate([taps_ref[span * PHASES + phase], taps_ref[(span + 1) * PHASES + phase]], axis=1)
            for phase in range(PHASES)
        ]
        out = jnp.dot(windows[...], jnp.concatenate(weights, axis=0), preferred_element_type=F32)
        for side in range(2):
            for row in range(rows // LANES):
                block = row - 1 + SPANS - (span + side)
                piece = out[row * LANES:(row + 1) * LANES, side * LANES:(side + 1) * LANES]
                cols = slice(block * LANES, (block + 1) * LANES)
                if block in seen:
                    total[cols, :] += piece
                else:
                    total[cols, :] = piece
                    seen.add(block)
    rows = kept_ref.shape[0]
    kept_ref[...] = total[pl.ds(pl.multiple_of(core_ref[0] * rows, rows), rows), :]
    sent_ref[...] = total[pl.ds(pl.multiple_of((1 - core_ref[0]) * rows, rows), rows), :]


def join_halves(core_ref, own_ref, other_ref, signal_t):
    rows = own_ref.shape[0]
    signal_t[pl.ds(pl.multiple_of(core_ref[0] * rows, rows), rows), :] = own_ref[...]
    signal_t[pl.ds(pl.multiple_of((1 - core_ref[0]) * rows, rows), rows), :] = other_ref[...]


def image_kernel(core_ref, taps_ref, own_ref, other_ref, part_ref, squares_ref, signal_t, packed):
    join_halves(core_ref, own_ref, other_ref, signal_t)
    result = forward_product(signal_t, taps_ref)
    gradient = signal_t[...]
    squares_ref[...] = jnp.sum(gradient * gradient, axis=0, keepdims=True)
    pack_strains(result, part_ref, packed)


def update_kernel(core_ref, forces_ref, own_ref, other_ref, image_ref, residual_ref, forces_out, residual_out, signal_t, packed):
    squares = image_ref[0, image_ref.shape[1] - 1]
    for chunk in range(1, image_ref.shape[0]):
        squares = squares + image_ref[chunk, image_ref.shape[1] - 1]
    squares = jnp.sum(squares, axis=1, keepdims=True)
    step_size = squares[1:2] / squares[0:1]
    unpack_strains(image_ref, packed)
    left = residual_ref[...] - step_size * packed[...]
    hots = residual_out.shape[0]
    left_t = jnp.concatenate([left[:, 0:hots], left[:, hots:2 * hots]], axis=0)
    residual_out[...] = left_t.T
    join_halves(core_ref, own_ref, other_ref, signal_t)
    for block in range(BLOCKS):
        cols = slice(block * LANES, (block + 1) * LANES)
        forces_out[:, cols] = forces_ref[:, cols].astype(F32) + step_size * signal_t[cols, :].T


def call(kernel, outs, scratch, operands):
    spaces = [pltpu.SMEM if operand.dtype == jnp.int32 else pltpu.VMEM for operand in operands]
    return pl.pallas_call(
        kernel,
        out_shape=outs,
        in_specs=[pl.BlockSpec(memory_space=space) for space in spaces],
        scratch_shapes=scratch,
        compiler_params=pltpu.CompilerParams(vmem_limit_bytes=VMEM_LIMIT),
    )(*operands)


def body(response, forces, measured):
    hots, loads, _ = response.shape
    load_axes = ("y", "zl")
    peers = lax.axis_size(load_axes)
    core = lax.axis_index("c").astype(jnp.int32).reshape(1)
    half = SEG_COLS // 2
    part = jax.ShapeDtypeStruct((peers, half // peers // GROUP, GROUP, LANES), F32)
    packed_shape = jax.ShapeDtypeStruct((half, 2 * hots), F32)
    core_shape = jax.ShapeDtypeStruct((COLS // 2, loads), F32)
    forward_scratch = [
        pltpu.VMEM((COLS, loads), F32),
        pltpu.VMEM((half, 2 * hots), F32),
    ]

    def spread(value, count):
        return jnp.broadcast_to(value[None], (count,) + value.shape)

    def scatter_sum(value, axis):
        return jnp.sum(lax.all_to_all(value, axis, 0, 0), axis=0)

    def gather(value, axis):
        return lax.all_to_all(spread(value, lax.axis_size(axis)), axis, 0, 0)

    def swapped(value, axis, pairs):
        return lax.ppermute(value, axis, pairs + [(b, a) for a, b in pairs])

    taps, core = lax.optimization_barrier((jnp.transpose(response, (2, 0, 1)), core))
    strain_part, measured_t = call(
        strain_kernel, (part, packed_shape), forward_scratch, (taps, forces, measured)
    )
    strains = gather(scatter_sum(strain_part, load_axes), load_axes)
    kept, sent, residual = call(
        gradient_kernel,
        (core_shape, core_shape, packed_shape),
        [
            pltpu.VMEM((half, 2 * hots), F32),
            pltpu.VMEM((SEG_COLS + 2 * LANES, 2 * hots), F32),
            pltpu.VMEM((SEG_COLS + LANES, PHASES * hots), BF16),
            pltpu.VMEM((COLS, loads), F32),
        ],
        (core, taps, strains, measured_t),
    )
    cores = [(0, 1)]
    own = kept + swapped(sent, "c", cores)
    own = scatter_sum(own.reshape(lax.axis_size("x"), -1, loads), "x")
    inner, outer = [(0, 1), (2, 3)], [(1, 2), (3, 0)]
    for even, odd in ((inner, outer), (outer, inner)):
        pairs = [(2 * i, 2 * j) for i, j in even] + [(2 * i + 1, 2 * j + 1) for i, j in odd]
        own = own + swapped(own, ("zh", "c"), pairs)
    own = gather(own, "x").reshape(COLS // 2, loads)
    other = swapped(own, "c", cores)
    image_part, own_squares = call(
        image_kernel, (part, jax.ShapeDtypeStruct((1, loads), F32)), forward_scratch, (core, taps, own, other)
    )
    image = scatter_sum(image_part, load_axes)
    squares = jnp.sum(image * image, axis=(0, 1))[None]
    squares = jnp.sum(gather(squares, ("zh", "x", "c")), axis=0)
    image, squares, own_squares = lax.optimization_barrier((image, squares, own_squares))
    extra = jnp.concatenate([squares, own_squares] * (GROUP // 2), axis=0)
    image = gather(jnp.concatenate([image, extra[None]], axis=0), load_axes)
    return call(
        update_kernel,
        (jax.ShapeDtypeStruct((loads, COLS), F32), jax.ShapeDtypeStruct((hots, SEG_COLS), F32)),
        [pltpu.VMEM((COLS, loads), F32), pltpu.VMEM((half, 2 * hots), F32)],
        (core, forces, own, other, image, residual),
    )


def solution(mesh):
    parts = Mesh(mesh.devices.reshape(4, 4, 2, 4, 4), ("zh", "x", "c", "zl", "y"))
    hot, load = ("zh", "x", "c"), ("zl", "y")
    return jax.shard_map(
        body,
        mesh=parts,
        in_specs=(P(hot, load, None), P(load, None), P(hot, None)),
        out_specs=(P(load, None), P(hot, None)),
        check_vma=False,
    )
```

```python
import jax
import jax.numpy as jnp
from jax import lax
from jax.experimental import pallas as pl
from jax.experimental.pallas import tpu as pltpu
from jax.sharding import Mesh, PartitionSpec as P

TAPS = 128
SEG = 48
CASES = 8
HIST = 128
STEPS = 176
LANES = 128
PHASES = LANES // CASES
SPANS = TAPS // PHASES
SEG_COLS = SEG * CASES
SEG_BLOCKS = SEG_COLS // LANES
COLS = STEPS * CASES
GROUP = 4
BLOCKS = COLS // LANES
F32 = jnp.float32
BF16 = jnp.bfloat16
VMEM_LIMIT = 40 * 1024 * 1024


def forward_product(signal_t, taps_ref):
    hots = taps_ref.shape[1]
    parts = [None] * SEG_BLOCKS
    for block in range(1, BLOCKS, 2):
        low = max(SPANS - 1 - block, 0)
        high = min(SPANS + 2 - block, SPANS - 1)
        first = block * LANES
        windows = [signal_t[first - CASES * phase:first - CASES * phase + 2 * LANES, :].astype(BF16) for phase in range(PHASES)]
        weights = [
            jnp.concatenate([taps_ref[span * PHASES + phase] for phase in range(PHASES)], axis=1)
            for span in range(low, high + 1)
        ]
        out = lax.dot_general(
            jnp.concatenate(windows, axis=1),
            jnp.concatenate(weights, axis=0),
            (((1,), (1,)), ((), ())),
            preferred_element_type=F32,
        )
        for half in range(2):
            for span in range(low, high + 1):
                target = block + half + span - SPANS
                if 0 <= target < SEG_BLOCKS:
                    piece = out[half * LANES:(half + 1) * LANES, (span - low) * hots:(span - low + 1) * hots]
                    parts[target] = piece if parts[target] is None else parts[target] + piece
    return jnp.concatenate(parts, axis=0)


def pack_strains(value, out_ref, scratch):
    half = SEG_COLS // 2
    hots = value.shape[1]
    scratch[:, 0:hots] = value[0:half]
    scratch[:, hots:2 * hots] = value[half:]
    groups = out_ref.shape[1]
    for group in range(half // GROUP):
        out_ref[group // groups, group % groups] = scratch[group * GROUP:(group + 1) * GROUP, :]


def unpack_strains(chunks_ref, scratch):
    half = SEG_COLS // 2
    groups = half // GROUP // chunks_ref.shape[0]
    for group in range(half // GROUP):
        scratch[group * GROUP:(group + 1) * GROUP, :] = chunks_ref[group // groups, group % groups]


def strain_kernel(taps_ref, forces_ref, measured_ref, part_ref, measured_t_ref, signal_t, packed):
    for block in range(BLOCKS):
        cols = slice(block * LANES, (block + 1) * LANES)
        signal_t[cols, :] = forces_ref[:, cols].astype(F32).T
    result = forward_product(signal_t, taps_ref)
    pack_strains(result, part_ref, packed)
    half = SEG_COLS // 2
    hots = measured_ref.shape[0]
    measured_t = measured_ref[...].T
    measured_t_ref[:, 0:hots] = measured_t[0:half]
    measured_t_ref[:, hots:2 * hots] = measured_t[half:]


def gradient_kernel(core_ref, taps_ref, strains_ref, measured_t_ref, kept_ref, sent_ref, residual_ref, packed, padded, windows, total):
    hots = taps_ref.shape[1]
    half = SEG_COLS // 2
    unpack_strains(strains_ref, packed)
    residual = measured_t_ref[...] - packed[...]
    residual_ref[...] = residual
    padded[...] = jnp.zeros_like(padded)
    for lane, shift in ((0, 0), (hots, CASES)):
        padded[LANES - shift:LANES - shift + half, lane:lane + hots] = residual[:, 0:hots]
        padded[LANES - shift + half:LANES - shift + 2 * half, lane:lane + hots] = residual[:, hots:2 * hots]
    rows = windows.shape[0]
    for pair in range(PHASES // 2):
        first = 2 * CASES * pair
        windows[:, pair * 2 * hots:(pair + 1) * 2 * hots] = padded[first:first + rows, :].astype(BF16)
    seen = set()
    for span in range(0, SPANS, 2):
        weights = [
            jnp.concatenate([taps_ref[span * PHASES + phase], taps_ref[(span + 1) * PHASES + phase]], axis=1)
            for phase in range(PHASES)
        ]
        out = jnp.dot(windows[...], jnp.concatenate(weights, axis=0), preferred_element_type=F32)
        for side in range(2):
            for row in range(rows // LANES):
                block = row - 1 + SPANS - (span + side)
                piece = out[row * LANES:(row + 1) * LANES, side * LANES:(side + 1) * LANES]
                cols = slice(block * LANES, (block + 1) * LANES)
                if block in seen:
                    total[cols, :] += piece
                else:
                    total[cols, :] = piece
                    seen.add(block)
    rows = kept_ref.shape[0]
    kept_ref[...] = total[pl.ds(pl.multiple_of(core_ref[0] * rows, rows), rows), :]
    sent_ref[...] = total[pl.ds(pl.multiple_of((1 - core_ref[0]) * rows, rows), rows), :]


def join_halves(core_ref, own_ref, other_ref, signal_t):
    rows = own_ref.shape[0]
    signal_t[pl.ds(pl.multiple_of(core_ref[0] * rows, rows), rows), :] = own_ref[...]
    signal_t[pl.ds(pl.multiple_of((1 - core_ref[0]) * rows, rows), rows), :] = other_ref[...]


def image_kernel(core_ref, taps_ref, own_ref, other_ref, part_ref, squares_ref, signal_t, packed):
    join_halves(core_ref, own_ref, other_ref, signal_t)
    result = forward_product(signal_t, taps_ref)
    gradient = signal_t[...]
    squares_ref[...] = jnp.sum(gradient * gradient, axis=0, keepdims=True)
    pack_strains(result, part_ref, packed)


def update_kernel(core_ref, forces_ref, own_ref, other_ref, image_ref, residual_ref, forces_out, residual_out, signal_t, packed):
    squares = image_ref[0, image_ref.shape[1] - 1]
    for chunk in range(1, image_ref.shape[0]):
        squares = squares + image_ref[chunk, image_ref.shape[1] - 1]
    squares = jnp.sum(squares, axis=1, keepdims=True)
    step_size = squares[1:2] / squares[0:1]
    unpack_strains(image_ref, packed)
    left = residual_ref[...] - step_size * packed[...]
    hots = residual_out.shape[0]
    left_t = jnp.concatenate([left[:, 0:hots], left[:, hots:2 * hots]], axis=0)
    residual_out[...] = left_t.T
    join_halves(core_ref, own_ref, other_ref, signal_t)
    for block in range(BLOCKS):
        cols = slice(block * LANES, (block + 1) * LANES)
        forces_out[:, cols] = forces_ref[:, cols].astype(F32) + step_size * signal_t[cols, :].T


def call(kernel, outs, scratch, operands):
    spaces = [pltpu.SMEM if operand.dtype == jnp.int32 else pltpu.VMEM for operand in operands]
    return pl.pallas_call(
        kernel,
        out_shape=outs,
        in_specs=[pl.BlockSpec(memory_space=space) for space in spaces],
        scratch_shapes=scratch,
        compiler_params=pltpu.CompilerParams(vmem_limit_bytes=VMEM_LIMIT),
    )(*operands)


def body(response, forces, measured):
    hots, loads, _ = response.shape
    load_axes = ("y", "zl")
    peers = lax.axis_size(load_axes)
    core = lax.axis_index("c").astype(jnp.int32).reshape(1)
    half = SEG_COLS // 2
    part = jax.ShapeDtypeStruct((peers, half // peers // GROUP, GROUP, LANES), F32)
    packed_shape = jax.ShapeDtypeStruct((half, 2 * hots), F32)
    core_shape = jax.ShapeDtypeStruct((COLS // 2, loads), F32)
    forward_scratch = [
        pltpu.VMEM((COLS, loads), F32),
        pltpu.VMEM((half, 2 * hots), F32),
    ]

    def spread(value, count):
        return jnp.broadcast_to(value[None], (count,) + value.shape)

    def scatter_sum(value, axis):
        return jnp.sum(lax.all_to_all(value, axis, 0, 0), axis=0)

    def gather(value, axis):
        return lax.all_to_all(spread(value, lax.axis_size(axis)), axis, 0, 0)

    def swapped(value, axis, pairs):
        return lax.ppermute(value, axis, pairs + [(b, a) for a, b in pairs])

    taps, core = lax.optimization_barrier((jnp.transpose(response, (2, 0, 1)), core))
    strain_part, measured_t = call(
        strain_kernel, (part, packed_shape), forward_scratch, (taps, forces, measured)
    )
    strains = gather(scatter_sum(strain_part, load_axes), load_axes)
    kept, sent, residual = call(
        gradient_kernel,
        (core_shape, core_shape, packed_shape),
        [
            pltpu.VMEM((half, 2 * hots), F32),
            pltpu.VMEM((SEG_COLS + 2 * LANES, 2 * hots), F32),
            pltpu.VMEM((SEG_COLS + LANES, PHASES * hots), BF16),
            pltpu.VMEM((COLS, loads), F32),
        ],
        (core, taps, strains, measured_t),
    )
    cores = [(0, 1)]
    own = kept + swapped(sent, "c", cores)
    own = scatter_sum(own.reshape(lax.axis_size("x"), -1, loads), "x")
    inner, outer = [(0, 1), (2, 3)], [(1, 2), (3, 0)]
    for even, odd in ((inner, outer), (outer, inner)):
        pairs = [(2 * i, 2 * j) for i, j in even] + [(2 * i + 1, 2 * j + 1) for i, j in odd]
        own = own + swapped(own, ("zh", "c"), pairs)
    own = gather(own, "x").reshape(COLS // 2, loads)
    other = swapped(own, "c", cores)
    image_part, own_squares = call(
        image_kernel, (part, jax.ShapeDtypeStruct((1, loads), F32)), forward_scratch, (core, taps, own, other)
    )
    image = scatter_sum(image_part, load_axes)
    squares = jnp.sum(image * image, axis=(0, 1))[None]
    squares = jnp.sum(gather(squares, ("x", "zh", "c")), axis=0)
    image, squares, own_squares = lax.optimization_barrier((image, squares, own_squares))
    extra = jnp.concatenate([squares, own_squares] * (GROUP // 2), axis=0)
    image = gather(jnp.concatenate([image, extra[None]], axis=0), load_axes)
    return call(
        update_kernel,
        (jax.ShapeDtypeStruct((loads, COLS), F32), jax.ShapeDtypeStruct((hots, SEG_COLS), F32)),
        [pltpu.VMEM((COLS, loads), F32), pltpu.VMEM((half, 2 * hots), F32)],
        (core, forces, own, other, image, residual),
    )


def solution(mesh):
    parts = Mesh(mesh.devices.reshape(4, 4, 2, 4, 4), ("zh", "x", "c", "zl", "y"))
    hot, load = ("zh", "x", "c"), ("zl", "y")
    return jax.shard_map(
        body,
        mesh=parts,
        in_specs=(P(hot, load, None), P(load, None), P(hot, None)),
        out_specs=(P(load, None), P(hot, None)),
        check_vma=False,
    )
```
